32 devices in a mesh: ex: 4 (over z), col: 4 (over y, core), lay: 2 (over x).
Axes of the slice: x: 2, y: 2, z: 4, core: 2. Of those that a mesh axis runs over, the one named last changes fastest.
Arguments:
- normalized: bfloat16 [256, 2, 4, 3584], P('ex', 'lay', None, 'col'), may hold values from -6 to 6
- upstream: bfloat16 [256, 2, 4, 3584], P('ex', 'lay', None, 'col'), may hold values from -3 to 3
- owner_order: int32 [4, 64], P('ex'), may hold values from 0 to 63, each once within a row
- sketch_index: int32 [2, 28, 4], P(None, 'col'), may hold values from 0 to 63, all different within a row
- sketch_scale: bfloat16 [2, 28, 4], P(None, 'col'), may hold values from -1.5 to 1.5
- query_sketch: bfloat16 [4, 8192], P('ex', 'col'), may hold values from -0.0625 to 0.0625
Outputs:
- sketch: bfloat16 [256, 8192], P(('ex', 'lay'), 'col')
- scores: float32 [256, 4], P(('ex', 'lay'), 'col')
The draws below stay inside these ranges and needn't reach their ends.
Inputs may be any that keep to these rules, and one draw needn't show every extreme that they name: Each row is an ordering of the 64 examples of one block; the example at place j of row g is training example g * 64 + owner_order[g, j]. `sketch_index`: the 4 output blocks of one input block are distinct; every output block is named by some input block.
All inputs are finite; a program needn't handle non-finite values.
Results may differ from the reference program's by a relative error of at most 0.0049.
Values may be sent and summed in bfloat16 or wider, within the bound.
A program may use at most 64 MiB of HBM per device.

```python
import math
import jax
import jax.numpy as jnp
from jax import lax

D = 3584
SKETCH = 8192
KS = 4
T_EX = 4
EX_DEV = 64
EXAMPLES = 256
LAYERS = 2
QUERIES = 4
GROUPS = 4
DB = 28
NB = 64


def levels(stream_key, dims, shards, low, top_value):
    def one(position, parts):
        draws = jax.random.uniform(jax.random.fold_in(jax.random.fold_in(stream_key, 6), position), (parts,), jnp.float32, low / len(shards), top_value / len(shards))
        return jnp.repeat(jnp.exp(draws), dims[position] // parts).reshape((-1,) + (1,) * (len(dims) - position - 1))

    gain = one(*shards[0])
    for cut in shards[1:]:
        gain = gain * one(*cut)
    return gain


def different_ones(stream_key, rows, number_of, top, lift):
    order = jax.random.permutation(jax.random.fold_in(stream_key, 1), number_of)
    boost = order
    for power in range(3):
        boost = boost * boost // number_of
    boost = boost * lift // number_of
    chance = jax.random.randint(jax.random.fold_in(stream_key, 2), (rows, number_of), 0, 4096) + boost
    holders = jax.random.permutation(jax.random.fold_in(stream_key, 3), rows)[jnp.arange(number_of) % rows]
    chance = jnp.where(jnp.arange(rows)[:, None] == holders[None, :], 1 << 14, chance)
    merit = chance * number_of + jnp.arange(number_of)
    return lax.top_k(merit.astype(jnp.int32), top)[1].astype(jnp.int32)


def normal_values(own_key, dims, width, limit, cuts=(), kind=jnp.bfloat16):
    loudness = levels(own_key, dims, cuts, -0.22, 0.18) if cuts else 1.0
    drawn = jax.random.normal(own_key, dims, jnp.float32) * width * loudness
    return jnp.minimum(jnp.maximum(drawn, -limit), limit).astype(kind)


def setup_inputs(seed: int = 0) -> dict:
    keys = jax.random.split(jax.random.key(seed), 7)
    return {
        "normalized": normal_values(keys[0], (EXAMPLES, LAYERS, T_EX, D), 1.0, 6.0, ((0, 4), (1, 2), (3, 4))),
        "upstream": normal_values(keys[1], (EXAMPLES, LAYERS, T_EX, D), 0.35, 3.0, ((0, 4), (1, 2), (3, 4))),
        "owner_order": jax.vmap(lambda own: jax.random.permutation(own, EX_DEV))(jax.random.split(keys[2], GROUPS)).reshape((GROUPS, EX_DEV)).astype(jnp.int32),
        "sketch_index": different_ones(keys[3], LAYERS * DB, NB, KS, 0).reshape((LAYERS, DB, KS)),
        "sketch_scale": normal_values(keys[4], (LAYERS, DB, KS), 0.25, 1.5, ((1, 4),)),
        "query_sketch": normal_values(keys[5], (QUERIES, SKETCH), SKETCH ** -0.5, 0.0625, ((0, 4), (1, 4))),
    }


def hadamard_table():
    counter = jnp.arange(128, dtype=jnp.int32)
    both = counter[:, None] & counter[None, :]
    parity = jnp.zeros((128, 128), jnp.int32)
    for shift_bit in range(7):
        parity = parity + (both >> shift_bit & 1)
    signs = 1 - 2 * (parity % 2)
    return signs.astype(jnp.float32) / math.sqrt(128.0)

def reference(normalized, upstream, owner_order, sketch_index, sketch_scale, query_sketch):

    def layer_grad(layer):
        left = lax.dynamic_index_in_dim(normalized, layer, 1, keepdims=False).astype(jnp.float32)
        right = lax.dynamic_index_in_dim(upstream, layer, 1, keepdims=False).astype(jnp.float32)
        return lax.optimization_barrier(jnp.sum(left * right, axis=1)).astype(jnp.bfloat16)
    per_layer = lax.map(layer_grad, jnp.arange(LAYERS, dtype=jnp.int32))
    grads = jnp.transpose(per_layer, (1, 0, 2))
    positions = jnp.arange(EXAMPLES, dtype=jnp.int32)
    order = positions // EX_DEV * EX_DEV + owner_order.reshape(-1).astype(jnp.int32)
    ordered = jnp.take(grads, order, axis=0)
    targets = jnp.arange(NB, dtype=jnp.int32)
    table = (sketch_index[..., None] == targets).astype(jnp.float32) * sketch_scale.astype(jnp.float32)[..., None]
    table = lax.optimization_barrier(jnp.sum(table, axis=2)).reshape(LAYERS * DB, NB)
    rows = ordered.reshape(EXAMPLES, LAYERS * DB, 128).astype(jnp.float32)
    mixed = jnp.einsum('ebc,bo->eoc', rows, table, precision=lax.Precision.HIGHEST)
    rotated = jnp.einsum('eoc,cd->eod', mixed, hadamard_table(), precision=lax.Precision.HIGHEST)
    sketch = rotated.reshape(EXAMPLES, SKETCH).astype(jnp.bfloat16)
    scores = jnp.einsum('ec,qc->eq', sketch.astype(jnp.float32), query_sketch.astype(jnp.float32), precision=lax.Precision.HIGHEST)
    return (sketch, scores)
```

```python
import functools
import math

import jax
import jax.numpy as jnp
from jax import lax
from jax.experimental import pallas as pl
from jax.experimental.pallas import tpu as pltpu
from jax.sharding import PartitionSpec as P

MESH = pl.DeviceIdType.MESH
LANES = 128
CHUNKS = 4


def signs():
    bits = lax.broadcasted_iota(jnp.int32, (LANES, LANES), 0) & lax.broadcasted_iota(
        jnp.int32, (LANES, LANES), 1
    )
    bits = bits ^ (bits >> 4)
    bits = bits ^ (bits >> 2)
    bits = bits ^ (bits >> 1)
    return (1 - 2 * (bits & 1)).astype(jnp.float32).astype(jnp.bfloat16)


def kernel(
    sizes,
    x_hbm,
    u_hbm,
    order_ref,
    index_ref,
    scale_ref,
    query_ref,
    sketch_ref,
    scores_ref,
    x_ref,
    u_ref,
    grads_ref,
    owned_ref,
    pieces_ref,
    own_tab_ref,
    tabs_ref,
    own_query_f32_ref,
    own_query_ref,
    queries_ref,
    had_ref,
    splat_ref,
    weights_ref,
    rot_ref,
    total_ref,
    score_total_ref,
    in_sem,
    piece_send,
    piece_recv,
    relay_send,
    tab_send,
    tab_recv,
    query_send,
    query_recv,
    local_sem,
):
    n_ex, n_col, n_lay, per_col, k_sel = sizes
    ex, col, lay = lax.axis_index("ex"), lax.axis_index("col"), lax.axis_index("lay")
    examples, tokens, features = x_ref.shape
    rows = examples // n_lay
    in_blocks = features // LANES
    layers = index_ref.shape[0]
    out_blocks = query_ref.shape[1] // LANES
    chunk = examples // CHUNKS
    sibling = col + 1 - 2 * lax.rem(col, 2)
    scale = 1.0 / math.sqrt(float(LANES))

    loads = []
    for i in range(CHUNKS):
        part = pl.ds(i * chunk, chunk)
        pair = [
            pltpu.make_async_copy(x_hbm.at[part], x_ref.at[part], in_sem.at[2 * i]),
            pltpu.make_async_copy(u_hbm.at[part], u_ref.at[part], in_sem.at[2 * i + 1]),
        ]
        for copy in pair:
            copy.start()
        loads.append(pair)

    barrier = pltpu.get_barrier_semaphore()
    for dl in range(n_lay):
        for dc in range(n_col):
            if dl or dc:
                pl.semaphore_signal(
                    barrier,
                    inc=1,
                    device_id={
                        "ex": ex,
                        "col": lax.rem(col + dc, n_col),
                        "lay": lax.rem(lay + dl, n_lay),
                    },
                    device_id_type=MESH,
                )
    for j in range(per_col):
        holder = col * per_col + j
        for other in range(n_col):

            @pl.when(holder != ex)
            def _():
                pl.semaphore_signal(
                    barrier,
                    inc=1,
                    device_id={"ex": holder, "col": other, "lay": lay},
                    device_id_type=MESH,
                )

    had_ref[...] = signs()
    own_tab_ref[...] = jnp.full(own_tab_ref.shape, -1.0, jnp.float32)
    for layer in range(layers):
        own_tab_ref[layer, 0:k_sel, 0:in_blocks] = index_ref[layer].astype(jnp.float32)
        own_tab_ref[layer, k_sel : 2 * k_sel, 0:in_blocks] = scale_ref[layer].astype(jnp.float32)
    for o in range(out_blocks):
        own_query_f32_ref[o : o + 1, :] = query_ref[:, o * LANES : (o + 1) * LANES].astype(
            jnp.float32
        )
    own_query_ref[...] = own_query_f32_ref[...].astype(jnp.bfloat16)

    pl.semaphore_wait(barrier, n_lay * n_col - 1 + n_ex - 1)

    def tab_copy(dc):
        return pltpu.make_async_remote_copy(
            src_ref=own_tab_ref,
            dst_ref=tabs_ref.at[col],
            send_sem=tab_send.at[dc],
            recv_sem=tab_recv.at[col],
            device_id={"ex": ex, "col": lax.rem(col + dc, n_col), "lay": lay},
            device_id_type=MESH,
        )

    tab_copies = [tab_copy(dc) for dc in range(1, n_col)]
    for copy in tab_copies:
        copy.start()

    asker = ex // per_col
    slot = lax.rem(ex, per_col)

    def query_copy(target):
        return pltpu.make_async_remote_copy(
            src_ref=own_query_ref,
            dst_ref=queries_ref.at[slot, col],
            send_sem=query_send.at[target],
            recv_sem=query_recv.at[slot, col],
            device_id={"ex": target, "col": asker, "lay": lay},
            device_id_type=MESH,
        )

    def keep_query():
        return pltpu.make_async_copy(
            own_query_ref, queries_ref.at[slot, col], query_recv.at[slot, col]
        )

    for target in range(n_ex):
        mine = jnp.logical_and(target == ex, asker == col)

        @pl.when(jnp.logical_not(mine))
        def _():
            query_copy(target).start()

        @pl.when(mine)
        def _():
            keep_query().start()

    for i in range(CHUNKS):
        for copy in loads[i]:
            copy.wait()
        part = slice(i * chunk, (i + 1) * chunk)
        grads_ref[part, :] = jnp.sum(
            x_ref[part].astype(jnp.float32) * u_ref[part].astype(jnp.float32), axis=1
        ).astype(jnp.bfloat16)
    chosen = (
        lax.broadcasted_iota(jnp.int32, (examples, examples), 0) == order_ref[...]
    ).astype(jnp.float32)
    chosen = chosen.T.astype(jnp.bfloat16)
    ordered = jnp.dot(chosen, grads_ref[...], preferred_element_type=jnp.float32)
    for owner in range(n_lay):
        owned_ref[owner] = ordered[owner * rows : (owner + 1) * rows].astype(jnp.bfloat16)

    offsets = [
        (dl, dc) for dl in range(n_lay) for dc in range(0, n_col, 2) if dl or dc
    ]
    offsets.sort(key=lambda at: (at[0] != 0) + (at[1] != 0))

    def piece_copy(number, dl, dc):
        to_lay, to_col = lax.rem(lay + dl, n_lay), lax.rem(col + dc, n_col)
        return pltpu.make_async_remote_copy(
            src_ref=owned_ref.at[to_lay],
            dst_ref=pieces_ref.at[lay, col],
            send_sem=piece_send.at[number],
            recv_sem=piece_recv.at[lay, col],
            device_id={"ex": ex, "col": to_col, "lay": to_lay},
            device_id_type=MESH,
        )

    def relay_copy(number, source, at_lay, at_col):
        return pltpu.make_async_remote_copy(
            src_ref=source,
            dst_ref=pieces_ref.at[at_lay, at_col],
            send_sem=relay_send.at[number],
            recv_sem=piece_recv.at[at_lay, at_col],
            device_id={"ex": ex, "col": sibling, "lay": lay},
            device_id_type=MESH,
        )

    def arrive(at_lay, at_col):
        pltpu.make_async_remote_copy(
            src_ref=owned_ref.at[0],
            dst_ref=pieces_ref.at[at_lay, at_col],
            send_sem=relay_send.at[0],
            recv_sem=piece_recv.at[at_lay, at_col],
            device_id={"ex": ex, "col": sibling, "lay": lay},
            device_id_type=MESH,
        ).wait_recv()

    sends = [piece_copy(n, dl, dc) for n, (dl, dc) in enumerate(offsets)]
    for copy in sends:
        copy.start()
    own_relay = relay_copy(len(offsets), owned_ref.at[lay], lay, col)
    own_relay.start()
    sends.append(own_relay)

    tabs_ref[col] = own_tab_ref[...]
    for dc in range(1, n_col):
        source = lax.rem(col + dc, n_col)
        pltpu.make_async_remote_copy(
            src_ref=own_tab_ref,
            dst_ref=tabs_ref.at[source],
            send_sem=tab_send.at[dc],
            recv_sem=tab_recv.at[source],
            device_id={"ex": ex, "col": source, "lay": lay},
            device_id_type=MESH,
        ).wait_recv()

    def table(at_lay, at_col, first, count):
        targets = (first + lax.broadcasted_iota(jnp.int32, (count, LANES), 0)).astype(jnp.float32)
        value = jnp.zeros((count, LANES), jnp.float32)
        for k in range(k_sel):
            index = tabs_ref[at_col, at_lay, k : k + 1, :]
            gain = tabs_ref[at_col, at_lay, k_sel + k : k_sel + k + 1, :]
            value = value + jnp.where(targets == index, gain, 0.0)
        return value

    for at_lay in range(layers):
        for at_col in range(n_col):
            mine = table(at_lay, at_col, col * out_blocks, out_blocks) * scale
            for b in range(in_blocks):
                splat_ref[at_lay, at_col, b] = jnp.broadcast_to(
                    mine[:, b : b + 1], (out_blocks, LANES)
                )

    def rotate(source):
        piece = source[...]
        stacked = jnp.concatenate(
            [piece[:, b * LANES : (b + 1) * LANES] for b in range(in_blocks)], axis=0
        )
        rot_ref[...] = jnp.dot(
            stacked, had_ref[...], preferred_element_type=jnp.float32
        ).reshape(in_blocks, rows, LANES)

    group = 4

    def combine(at_lay, at_col, first, last):
        for o in range(0, out_blocks, group):
            if first:
                sums = [jnp.zeros((rows, LANES), jnp.float32) for _ in range(group)]
            else:
                sums = [total_ref[o + g] for g in range(group)]
            for b in range(in_blocks):
                turned = rot_ref[b]
                for g in range(group):
                    sums[g] = sums[g] + turned * splat_ref[at_lay, at_col, b, o + g : o + g + 1, :]
            for g in range(group):
                if last:
                    sketch_ref[:, (o + g) * LANES : (o + g + 1) * LANES] = sums[g].astype(
                        jnp.bfloat16
                    )
                else:
                    total_ref[o + g] = sums[g]

    def score(at_lay, at_col, first, last):
        for q in range(per_col):
            if first:
                sums = jnp.zeros((rows, LANES), jnp.float32)
            else:
                sums = score_total_ref[q]
            for b in range(in_blocks):
                sums = sums + rot_ref[b] * weights_ref[
                    at_lay, at_col, b : b + 1, q * LANES : (q + 1) * LANES
                ]
            if last:
                scores_ref[:, q : q + 1] = jnp.sum(sums, axis=1, keepdims=True) * scale
            else:
                score_total_ref[q] = sums

    rotate(owned_ref.at[lay])
    combine(lay, col, True, False)

    for j in range(per_col):
        holder = col * per_col + j
        for other in range(n_col):
            here = jnp.logical_and(holder == ex, other == col)

            @pl.when(jnp.logical_not(here))
            def _():
                pltpu.make_async_remote_copy(
                    src_ref=own_query_ref,
                    dst_ref=queries_ref.at[j, other],
                    send_sem=query_send.at[0],
                    recv_sem=query_recv.at[j, other],
                    device_id={"ex": holder, "col": other, "lay": lay},
                    device_id_type=MESH,
                ).wait_recv()

            @pl.when(here)
            def _():
                keep_query().wait()

    asked = jnp.concatenate(
        [
            queries_ref[j].astype(jnp.float32).reshape(n_col * out_blocks, LANES)
            for j in range(per_col)
        ],
        axis=1,
    ).astype(jnp.bfloat16)
    for at_lay in range(layers):
        for at_col in range(n_col):
            whole = table(at_lay, at_col, 0, n_col * out_blocks).T.astype(jnp.bfloat16)
            weights_ref[at_lay, at_col] = jnp.dot(
                whole[0 : weights_ref.shape[2]], asked, preferred_element_type=jnp.float32
            )
    score(lay, col, True, False)

    arrive(lay, sibling)
    rotate(pieces_ref.at[lay, sibling])
    combine(lay, sibling, False, False)
    score(lay, sibling, False, False)
    relays = []
    for number, (dl, dc) in enumerate(offsets):
        at_lay, at_col = lax.rem(lay + dl, n_lay), lax.rem(col + dc, n_col)
        arrive(at_lay, at_col)
        relay = relay_copy(number, pieces_ref.at[at_lay, at_col], at_lay, at_col)
        relay.start()
        relays.append(relay)
        rotate(pieces_ref.at[at_lay, at_col])
        combine(at_lay, at_col, False, False)
        score(at_lay, at_col, False, False)
    for number, (dl, dc) in enumerate(offsets):
        at_lay, at_col = lax.rem(lay + dl, n_lay), lax.rem(sibling + dc, n_col)
        last = number == len(offsets) - 1
        arrive(at_lay, at_col)
        rotate(pieces_ref.at[at_lay, at_col])
        combine(at_lay, at_col, False, last)
        score(at_lay, at_col, False, last)

    for copy in sends + relays + tab_copies:
        copy.wait_send()
    for target in range(n_ex):
        mine = jnp.logical_and(target == ex, asker == col)

        @pl.when(jnp.logical_not(mine))
        def _():
            query_copy(target).wait_send()


def solution(mesh):
    n_ex, n_col, n_lay = (mesh.shape[name] for name in ("ex", "col", "lay"))

    def local(normalized, upstream, owner_order, sketch_index, sketch_scale, query_sketch):
        examples, own_layers, tokens, features = normalized.shape
        assert own_layers == 1
        layers, in_blocks, k_sel = sketch_index.shape
        width = query_sketch.shape[1]
        out_blocks = width // LANES
        per_col = n_ex * query_sketch.shape[0] // n_col
        rows = examples // n_lay
        padded = -(-in_blocks // 8) * 8
        vmem = pl.BlockSpec(memory_space=pltpu.VMEM)
        dma = pltpu.SemaphoreType.DMA
        return pl.pallas_call(
            functools.partial(kernel, (n_ex, n_col, n_lay, per_col, k_sel)),
            out_shape=(
                jax.ShapeDtypeStruct((rows, width), jnp.bfloat16),
                jax.ShapeDtypeStruct((rows, per_col), jnp.float32),
            ),
            in_specs=[pl.BlockSpec(memory_space=pl.ANY)] * 2 + [vmem] * 4,
            out_specs=(vmem, vmem),
            scratch_shapes=[
                pltpu.VMEM((examples, tokens, features), jnp.bfloat16),
                pltpu.VMEM((examples, tokens, features), jnp.bfloat16),
                pltpu.VMEM((examples, features), jnp.bfloat16),
                pltpu.VMEM((n_lay, rows, features), jnp.bfloat16),
                pltpu.VMEM((n_lay, n_col, rows, features), jnp.bfloat16),
                pltpu.VMEM((layers, 2 * k_sel, LANES), jnp.float32),
                pltpu.VMEM((n_col, layers, 2 * k_sel, LANES), jnp.float32),
                pltpu.VMEM((out_blocks, LANES), jnp.float32),
                pltpu.VMEM((out_blocks, LANES), jnp.bfloat16),
                pltpu.VMEM((per_col, n_col, out_blocks, LANES), jnp.bfloat16),
                pltpu.VMEM((LANES, LANES), jnp.bfloat16),
                pltpu.VMEM((layers, n_col, in_blocks, out_blocks, LANES), jnp.float32),
                pltpu.VMEM((layers, n_col, padded, per_col * LANES), jnp.float32),
                pltpu.VMEM((in_blocks, rows, LANES), jnp.float32),
                pltpu.VMEM((out_blocks, rows, LANES), jnp.float32),
                pltpu.VMEM((per_col, rows, LANES), jnp.float32),
                dma((2 * CHUNKS,)),
                dma((n_lay * n_col,)),
                dma((n_lay, n_col)),
                dma((n_lay * n_col,)),
                dma((n_col,)),
                dma((n_col,)),
                dma((n_ex,)),
                dma((per_col, n_col)),
                dma((1,)),
            ],
            compiler_params=pltpu.CompilerParams(collective_id=0, has_side_effects=True),
        )(
            normalized.reshape(examples, tokens, features),
            upstream.reshape(examples, tokens, features),
            owner_order,
            jnp.swapaxes(sketch_index, 1, 2),
            jnp.swapaxes(sketch_scale, 1, 2),
            query_sketch,
        )

    placed = (
        P("ex", "lay", None, "col"),
        P("ex", "lay", None, "col"),
        P("ex", None),
        P(None, "col", None),
        P(None, "col", None),
        P("ex", "col"),
    )
    return jax.shard_map(
        local,
        mesh=mesh,
        in_specs=placed,
        out_specs=(P(("ex", "lay"), "col"), P(("ex", "lay"), "col")),
        check_vma=False,
    )
```

```python
import functools
import math

import jax
import jax.numpy as jnp
from jax import lax
from jax.experimental import pallas as pl
from jax.experimental.pallas import tpu as pltpu
from jax.sharding import PartitionSpec as P

MESH = pl.DeviceIdType.MESH
LANES = 128
CHUNKS = 4


def signs():
    bits = lax.broadcasted_iota(jnp.int32, (LANES, LANES), 0) & lax.broadcasted_iota(
        jnp.int32, (LANES, LANES), 1
    )
    bits = bits ^ (bits >> 4)
    bits = bits ^ (bits >> 2)
    bits = bits ^ (bits >> 1)
    return (1 - 2 * (bits & 1)).astype(jnp.float32).astype(jnp.bfloat16)


def kernel(
    sizes,
    x_hbm,
    u_hbm,
    order_hbm,
    index_hbm,
    scale_hbm,
    query_hbm,
    sketch_ref,
    scores_ref,
    order_ref,
    index_ref,
    scale_ref,
    query_ref,
    x_ref,
    u_ref,
    grads_ref,
    owned_ref,
    pieces_ref,
    own_tab_ref,
    tabs_ref,
    own_query_f32_ref,
    own_query_ref,
    queries_ref,
    had_ref,
    splat_ref,
    weights_ref,
    rot_ref,
    total_ref,
    score_total_ref,
    in_sem,
    small_sem,
    piece_send,
    piece_recv,
    relay_send,
    tab_send,
    tab_recv,
    query_send,
    query_recv,
    local_sem,
):
    n_ex, n_col, n_lay, per_col, k_sel = sizes
    ex, col, lay = lax.axis_index("ex"), lax.axis_index("col"), lax.axis_index("lay")
    examples, tokens, features = x_ref.shape
    rows = examples // n_lay
    in_blocks = features // LANES
    layers = index_ref.shape[0]
    out_blocks = query_ref.shape[1] // LANES
    chunk = examples // CHUNKS
    sibling = col + 1 - 2 * lax.rem(col, 2)
    scale = 1.0 / math.sqrt(float(LANES))

    loads = []
    for i in range(CHUNKS):
        part = pl.ds(i * chunk, chunk)
        pair = [
            pltpu.make_async_copy(x_hbm.at[part], x_ref.at[part], in_sem.at[2 * i]),
            pltpu.make_async_copy(u_hbm.at[part], u_ref.at[part], in_sem.at[2 * i + 1]),
        ]
        for copy in pair:
            copy.start()
        loads.append(pair)

    smalls = [
        pltpu.make_async_copy(source, held, small_sem.at[i])
        for i, (source, held) in enumerate(
            [
                (query_hbm, query_ref),
                (index_hbm, index_ref),
                (scale_hbm, scale_ref),
                (order_hbm, order_ref),
            ]
        )
    ]
    for copy in smalls:
        copy.start()

    barrier = pltpu.get_barrier_semaphore()
    for dl in range(n_lay):
        for dc in range(n_col):
            if dl or dc:
                pl.semaphore_signal(
                    barrier,
                    inc=1,
                    device_id={
                        "ex": ex,
                        "col": lax.rem(col + dc, n_col),
                        "lay": lax.rem(lay + dl, n_lay),
                    },
                    device_id_type=MESH,
                )
    for j in range(per_col):
        holder = col * per_col + j
        for other in range(n_col):

            @pl.when(holder != ex)
            def _():
                pl.semaphore_signal(
                    barrier,
                    inc=1,
                    device_id={"ex": holder, "col": other, "lay": lay},
                    device_id_type=MESH,
                )

    had_ref[...] = signs()
    for copy in smalls:
        copy.wait()
    own_tab_ref[...] = jnp.full(own_tab_ref.shape, -1.0, jnp.float32)
    for layer in range(layers):
        own_tab_ref[layer, 0:k_sel, 0:in_blocks] = index_ref[layer].astype(jnp.float32)
        own_tab_ref[layer, k_sel : 2 * k_sel, 0:in_blocks] = scale_ref[layer].astype(jnp.float32)
    for o in range(out_blocks):
        own_query_f32_ref[o : o + 1, :] = query_ref[:, o * LANES : (o + 1) * LANES].astype(
            jnp.float32
        )
    own_query_ref[...] = own_query_f32_ref[...].astype(jnp.bfloat16)

    for i in range(CHUNKS):
        for copy in loads[i]:
            copy.wait()
        part = slice(i * chunk, (i + 1) * chunk)
        grads_ref[part, :] = jnp.sum(
            x_ref[part].astype(jnp.float32) * u_ref[part].astype(jnp.float32), axis=1
        ).astype(jnp.bfloat16)
    chosen = (
        lax.broadcasted_iota(jnp.int32, (examples, examples), 0) == order_ref[...]
    ).astype(jnp.float32)
    chosen = chosen.T.astype(jnp.bfloat16)
    ordered = jnp.dot(chosen, grads_ref[...], preferred_element_type=jnp.float32)
    for owner in range(n_lay):
        owned_ref[owner] = ordered[owner * rows : (owner + 1) * rows].astype(jnp.bfloat16)

    pl.semaphore_wait(barrier, n_lay * n_col - 1 + n_ex - 1)

    def tab_copy(dc):
        return pltpu.make_async_remote_copy(
            src_ref=own_tab_ref,
            dst_ref=tabs_ref.at[col],
            send_sem=tab_send.at[dc],
            recv_sem=tab_recv.at[col],
            device_id={"ex": ex, "col": lax.rem(col + dc, n_col), "lay": lay},
            device_id_type=MESH,
        )

    tab_copies = [tab_copy(dc) for dc in range(1, n_col)]
    for copy in tab_copies:
        copy.start()

    asker = ex // per_col
    slot = lax.rem(ex, per_col)

    def query_copy(target):
        return pltpu.make_async_remote_copy(
            src_ref=own_query_ref,
            dst_ref=queries_ref.at[slot, col],
            send_sem=query_send.at[target],
            recv_sem=query_recv.at[slot, col],
            device_id={"ex": target, "col": asker, "lay": lay},
            device_id_type=MESH,
        )

    def keep_query():
        return pltpu.make_async_copy(
            own_query_ref, queries_ref.at[slot, col], query_recv.at[slot, col]
        )

    for target in range(n_ex):
        mine = jnp.logical_and(target == ex, asker == col)

        @pl.when(jnp.logical_not(mine))
        def _():
            query_copy(target).start()

        @pl.when(mine)
        def _():
            keep_query().start()

    offsets = [
        (dl, dc) for dl in range(n_lay) for dc in range(0, n_col, 2) if dl or dc
    ]
    offsets.sort(key=lambda at: (at[0] != 0) + (at[1] != 0))

    def piece_copy(number, dl, dc):
        to_lay, to_col = lax.rem(lay + dl, n_lay), lax.rem(col + dc, n_col)
        return pltpu.make_async_remote_copy(
            src_ref=owned_ref.at[to_lay],
            dst_ref=pieces_ref.at[lay, col],
            send_sem=piece_send.at[number],
            recv_sem=piece_recv.at[lay, col],
            device_id={"ex": ex, "col": to_col, "lay": to_lay},
            device_id_type=MESH,
        )

    def relay_copy(number, source, at_lay, at_col):
        return pltpu.make_async_remote_copy(
            src_ref=source,
            dst_ref=pieces_ref.at[at_lay, at_col],
            send_sem=relay_send.at[number],
            recv_sem=piece_recv.at[at_lay, at_col],
            device_id={"ex": ex, "col": sibling, "lay": lay},
            device_id_type=MESH,
        )

    def arrive(at_lay, at_col):
        pltpu.make_async_remote_copy(
            src_ref=owned_ref.at[0],
            dst_ref=pieces_ref.at[at_lay, at_col],
            send_sem=relay_send.at[0],
            recv_sem=piece_recv.at[at_lay, at_col],
            device_id={"ex": ex, "col": sibling, "lay": lay},
            device_id_type=MESH,
        ).wait_recv()

    sends = [piece_copy(n, dl, dc) for n, (dl, dc) in enumerate(offsets)]
    for copy in sends:
        copy.start()
    own_relay = relay_copy(len(offsets), owned_ref.at[lay], lay, col)
    own_relay.start()
    sends.append(own_relay)

    tabs_ref[col] = own_tab_ref[...]
    for dc in range(1, n_col):
        source = lax.rem(col + dc, n_col)
        pltpu.make_async_remote_copy(
            src_ref=own_tab_ref,
            dst_ref=tabs_ref.at[source],
            send_sem=tab_send.at[dc],
            recv_sem=tab_recv.at[source],
            device_id={"ex": ex, "col": source, "lay": lay},
            device_id_type=MESH,
        ).wait_recv()

    def table(at_lay, at_col, first, count):
        targets = (first + lax.broadcasted_iota(jnp.int32, (count, LANES), 0)).astype(jnp.float32)
        value = jnp.zeros((count, LANES), jnp.float32)
        for k in range(k_sel):
            index = tabs_ref[at_col, at_lay, k : k + 1, :]
            gain = tabs_ref[at_col, at_lay, k_sel + k : k_sel + k + 1, :]
            value = value + jnp.where(targets == index, gain, 0.0)
        return value

    for at_lay in range(layers):
        for at_col in range(n_col):
            mine = table(at_lay, at_col, col * out_blocks, out_blocks) * scale
            for b in range(in_blocks):
                splat_ref[at_lay, at_col, b] = jnp.broadcast_to(
                    mine[:, b : b + 1], (out_blocks, LANES)
                )

    def rotate(source):
        piece = source[...]
        stacked = jnp.concatenate(
            [piece[:, b * LANES : (b + 1) * LANES] for b in range(in_blocks)], axis=0
        )
        rot_ref[...] = jnp.dot(
            stacked, had_ref[...], preferred_element_type=jnp.float32
        ).reshape(in_blocks, rows, LANES)

    group = 4

    def combine(at_lay, at_col, first, last):
        for o in range(0, out_blocks, group):
            if first:
                sums = [jnp.zeros((rows, LANES), jnp.float32) for _ in range(group)]
            else:
                sums = [total_ref[o + g] for g in range(group)]
            for b in range(in_blocks):
                turned = rot_ref[b]
                for g in range(group):
                    sums[g] = sums[g] + turned * splat_ref[at_lay, at_col, b, o + g : o + g + 1, :]
            for g in range(group):
                if last:
                    sketch_ref[:, (o + g) * LANES : (o + g + 1) * LANES] = sums[g].astype(
                        jnp.bfloat16
                    )
                else:
                    total_ref[o + g] = sums[g]

    def score(at_lay, at_col, first, last):
        for q in range(per_col):
            if first:
                sums = jnp.zeros((rows, LANES), jnp.float32)
            else:
                sums = score_total_ref[q]
            for b in range(in_blocks):
                sums = sums + rot_ref[b] * weights_ref[
                    at_lay, at_col, b : b + 1, q * LANES : (q + 1) * LANES
                ]
            if last:
                scores_ref[q : q + 1, :] = jnp.sum(sums.T, axis=0, keepdims=True) * scale
            else:
                score_total_ref[q] = sums

    rotate(owned_ref.at[lay])
    combine(lay, col, True, False)

    for j in range(per_col):
        holder = col * per_col + j
        for other in range(n_col):
            here = jnp.logical_and(holder == ex, other == col)

            @pl.when(jnp.logical_not(here))
            def _():
                pltpu.make_async_remote_copy(
                    src_ref=own_query_ref,
                    dst_ref=queries_ref.at[j, other],
                    send_sem=query_send.at[0],
                    recv_sem=query_recv.at[j, other],
                    device_id={"ex": holder, "col": other, "lay": lay},
                    device_id_type=MESH,
                ).wait_recv()

            @pl.when(here)
            def _():
                keep_query().wait()

    asked = jnp.concatenate(
        [
            queries_ref[j].astype(jnp.float32).reshape(n_col * out_blocks, LANES)
            for j in range(per_col)
        ],
        axis=1,
    ).astype(jnp.bfloat16)
    for at_lay in range(layers):
        for at_col in range(n_col):
            whole = table(at_lay, at_col, 0, n_col * out_blocks).T.astype(jnp.bfloat16)
            weights_ref[at_lay, at_col] = jnp.dot(
                whole[0 : weights_ref.shape[2]], asked, preferred_element_type=jnp.float32
            )
    score(lay, col, True, False)

    arrive(lay, sibling)
    rotate(pieces_ref.at[lay, sibling])
    combine(lay, sibling, False, False)
    score(lay, sibling, False, False)
    relays = []
    for number, (dl, dc) in enumerate(offsets):
        at_lay, at_col = lax.rem(lay + dl, n_lay), lax.rem(col + dc, n_col)
        arrive(at_lay, at_col)
        relay = relay_copy(number, pieces_ref.at[at_lay, at_col], at_lay, at_col)
        relay.start()
        relays.append(relay)
        rotate(pieces_ref.at[at_lay, at_col])
        combine(at_lay, at_col, False, False)
        score(at_lay, at_col, False, False)
    for number, (dl, dc) in enumerate(offsets):
        at_lay, at_col = lax.rem(lay + dl, n_lay), lax.rem(sibling + dc, n_col)
        last = number == len(offsets) - 1
        arrive(at_lay, at_col)
        rotate(pieces_ref.at[at_lay, at_col])
        combine(at_lay, at_col, False, last)
        score(at_lay, at_col, False, last)

    for copy in sends + relays + tab_copies:
        copy.wait_send()
    for target in range(n_ex):
        mine = jnp.logical_and(target == ex, asker == col)

        @pl.when(jnp.logical_not(mine))
        def _():
            query_copy(target).wait_send()


def solution(mesh):
    n_ex, n_col, n_lay = (mesh.shape[name] for name in ("ex", "col", "lay"))

    def local(normalized, upstream, owner_order, sketch_index, sketch_scale, query_sketch):
        examples, own_layers, tokens, features = normalized.shape
        assert own_layers == 1
        layers, in_blocks, k_sel = sketch_index.shape
        width = query_sketch.shape[1]
        out_blocks = width // LANES
        per_col = n_ex * query_sketch.shape[0] // n_col
        rows = examples // n_lay
        padded = -(-in_blocks // 8) * 8
        vmem = pl.BlockSpec(memory_space=pltpu.VMEM)
        dma = pltpu.SemaphoreType.DMA
        sketch, scores = pl.pallas_call(
            functools.partial(kernel, (n_ex, n_col, n_lay, per_col, k_sel)),
            out_shape=(
                pltpu.VMEM((rows, width), jnp.bfloat16),
                pltpu.VMEM((per_col, rows), jnp.float32),
            ),
            in_specs=[pl.BlockSpec(memory_space=pl.ANY)] * 6,
            out_specs=(vmem, vmem),
            scratch_shapes=[
                pltpu.VMEM(owner_order.shape, jnp.int32),
                pltpu.VMEM((layers, k_sel, in_blocks), jnp.int32),
                pltpu.VMEM((layers, k_sel, in_blocks), jnp.bfloat16),
                pltpu.VMEM(query_sketch.shape, jnp.bfloat16),
                pltpu.VMEM((examples, tokens, features), jnp.bfloat16),
                pltpu.VMEM((examples, tokens, features), jnp.bfloat16),
                pltpu.VMEM((examples, features), jnp.bfloat16),
                pltpu.VMEM((n_lay, rows, features), jnp.bfloat16),
                pltpu.VMEM((n_lay, n_col, rows, features), jnp.bfloat16),
                pltpu.VMEM((layers, 2 * k_sel, LANES), jnp.float32),
                pltpu.VMEM((n_col, layers, 2 * k_sel, LANES), jnp.float32),
                pltpu.VMEM((out_blocks, LANES), jnp.float32),
                pltpu.VMEM((out_blocks, LANES), jnp.bfloat16),
                pltpu.VMEM((per_col, n_col, out_blocks, LANES), jnp.bfloat16),
                pltpu.VMEM((LANES, LANES), jnp.bfloat16),
                pltpu.VMEM((layers, n_col, in_blocks, out_blocks, LANES), jnp.float32),
                pltpu.VMEM((layers, n_col, padded, per_col * LANES), jnp.float32),
                pltpu.VMEM((in_blocks, rows, LANES), jnp.float32),
                pltpu.VMEM((out_blocks, rows, LANES), jnp.float32),
                pltpu.VMEM((per_col, rows, LANES), jnp.float32),
                dma((2 * CHUNKS,)),
                dma((4,)),
                dma((n_lay * n_col,)),
                dma((n_lay, n_col)),
                dma((n_lay * n_col,)),
                dma((n_col,)),
                dma((n_col,)),
                dma((n_ex,)),
                dma((per_col, n_col)),
                dma((1,)),
            ],
            compiler_params=pltpu.CompilerParams(collective_id=0, has_side_effects=True),
        )(
            normalized.reshape(examples, tokens, features),
            upstream.reshape(examples, tokens, features),
            owner_order,
            jnp.swapaxes(sketch_index, 1, 2),
            jnp.swapaxes(sketch_scale, 1, 2),
            query_sketch,
        )
        return sketch, scores.T

    placed = (
        P("ex", "lay", None, "col"),
        P("ex", "lay", None, "col"),
        P("ex", None),
        P(None, "col", None),
        P(None, "col", None),
        P("ex", "col"),
    )
    return jax.shard_map(
        local,
        mesh=mesh,
        in_specs=placed,
        out_specs=(P(("ex", "lay"), "col"), P(("ex", "lay"), "col")),
        check_vma=False,
    )
```

```python
import functools
import math

import jax
import jax.numpy as jnp
from jax import lax
from jax.experimental import pallas as pl
from jax.experimental.pallas import tpu as pltpu
from jax.sharding import PartitionSpec as P

MESH = pl.DeviceIdType.MESH
LANES = 128
CHUNKS = 4


def signs():
    bits = lax.broadcasted_iota(jnp.int32, (LANES, LANES), 0) & lax.broadcasted_iota(
        jnp.int32, (LANES, LANES), 1
    )
    bits = bits ^ (bits >> 4)
    bits = bits ^ (bits >> 2)
    bits = bits ^ (bits >> 1)
    return (1 - 2 * (bits & 1)).astype(jnp.float32).astype(jnp.bfloat16)


def kernel(
    sizes,
    x_hbm,
    u_hbm,
    order_hbm,
    index_hbm,
    scale_hbm,
    query_hbm,
    sketch_ref,
    scores_ref,
    order_ref,
    index_ref,
    scale_ref,
    query_ref,
    x_ref,
    u_ref,
    grads_ref,
    owned_ref,
    pieces_ref,
    own_tab_ref,
    tabs_ref,
    own_query_f32_ref,
    own_query_ref,
    queries_ref,
    had_ref,
    splat_ref,
    turned_tab_ref,
    weights_ref,
    rot_ref,
    total_ref,
    in_sem,
    small_sem,
    piece_send,
    piece_recv,
    relay_send,
    tab_send,
    tab_recv,
    query_send,
    query_recv,
    ready_sem,
):
    n_ex, n_col, n_lay, per_col, k_sel = sizes
    ex, col, lay = lax.axis_index("ex"), lax.axis_index("col"), lax.axis_index("lay")
    examples, tokens, features = x_ref.shape
    rows = examples // n_lay
    in_blocks = features // LANES
    layers = index_ref.shape[0]
    out_blocks = query_ref.shape[1] // LANES
    padded = weights_ref.shape[2]
    chunk = examples // CHUNKS
    sibling = col + 1 - 2 * lax.rem(col, 2)
    scale = 1.0 / math.sqrt(float(LANES))

    loads = []
    for i in range(CHUNKS):
        part = pl.ds(i * chunk, chunk)
        pair = [
            pltpu.make_async_copy(x_hbm.at[part], x_ref.at[part], in_sem.at[2 * i]),
            pltpu.make_async_copy(u_hbm.at[part], u_ref.at[part], in_sem.at[2 * i + 1]),
        ]
        for copy in pair:
            copy.start()
        loads.append(pair)

    smalls = [
        pltpu.make_async_copy(source, held, small_sem.at[i])
        for i, (source, held) in enumerate(
            [
                (query_hbm, query_ref),
                (index_hbm, index_ref),
                (scale_hbm, scale_ref),
                (order_hbm, order_ref),
            ]
        )
    ]
    for copy in smalls:
        copy.start()

    barrier = pltpu.get_barrier_semaphore()
    for dl in range(n_lay):
        for dc in range(n_col):
            if dl or dc:
                pl.semaphore_signal(
                    barrier,
                    inc=1,
                    device_id={
                        "ex": ex,
                        "col": lax.rem(col + dc, n_col),
                        "lay": lax.rem(lay + dl, n_lay),
                    },
                    device_id_type=MESH,
                )
    has_lower, has_upper = ex > 0, ex < n_ex - 1

    def signal_plane(sem, step):
        pl.semaphore_signal(
            sem,
            inc=1,
            device_id={"ex": ex + step, "col": col, "lay": lay},
            device_id_type=MESH,
        )

    pl.when(has_lower)(lambda: signal_plane(barrier, -1))
    pl.when(has_upper)(lambda: signal_plane(barrier, 1))

    had_ref[...] = signs()
    for copy in smalls:
        copy.wait()
    own_tab_ref[...] = jnp.full(own_tab_ref.shape, -1.0, jnp.float32)
    for layer in range(layers):
        own_tab_ref[layer, 0:k_sel, 0:in_blocks] = index_ref[layer].astype(jnp.float32)
        own_tab_ref[layer, k_sel : 2 * k_sel, 0:in_blocks] = scale_ref[layer].astype(jnp.float32)
    for o in range(out_blocks):
        own_query_f32_ref[o : o + 1, :] = query_ref[:, o * LANES : (o + 1) * LANES].astype(
            jnp.float32
        )
    own_query_ref[...] = own_query_f32_ref[...].astype(jnp.bfloat16)

    for i in range(CHUNKS):
        for copy in loads[i]:
            copy.wait()
        part = slice(i * chunk, (i + 1) * chunk)
        grads_ref[part, :] = jnp.sum(
            x_ref[part].astype(jnp.float32) * u_ref[part].astype(jnp.float32), axis=1
        ).astype(jnp.bfloat16)
    chosen = (
        lax.broadcasted_iota(jnp.int32, (examples, examples), 0) == order_ref[...]
    ).astype(jnp.float32)
    chosen = chosen.T.astype(jnp.bfloat16)
    ordered = jnp.dot(chosen, grads_ref[...], preferred_element_type=jnp.float32)
    for owner in range(n_lay):
        owned_ref[owner] = ordered[owner * rows : (owner + 1) * rows].astype(jnp.bfloat16)

    planes = has_lower.astype(jnp.int32) + has_upper.astype(jnp.int32)
    pl.semaphore_wait(barrier, n_lay * n_col - 1 + planes)
    pl.when(jnp.logical_not(has_lower))(lambda: signal_plane(ready_sem.at[0], 1))
    pl.when(jnp.logical_not(has_upper))(lambda: signal_plane(ready_sem.at[1], -1))

    def tab_copy(dc):
        return pltpu.make_async_remote_copy(
            src_ref=own_tab_ref,
            dst_ref=tabs_ref.at[col],
            send_sem=tab_send.at[dc],
            recv_sem=tab_recv.at[col],
            device_id={"ex": ex, "col": lax.rem(col + dc, n_col), "lay": lay},
            device_id_type=MESH,
        )

    tab_copies = [tab_copy(dc) for dc in range(1, n_col)]
    for copy in tab_copies:
        copy.start()

    asker = ex // per_col
    slot = lax.rem(ex, per_col)

    def query_copy(target):
        return pltpu.make_async_remote_copy(
            src_ref=own_query_ref,
            dst_ref=queries_ref.at[slot, col],
            send_sem=query_send.at[target],
            recv_sem=query_recv.at[slot, col],
            device_id={"ex": target, "col": asker, "lay": lay},
            device_id_type=MESH,
        )

    def keep_query():
        return pltpu.make_async_copy(
            own_query_ref, queries_ref.at[slot, col], query_recv.at[slot, col]
        )

    def send_query(target, wanted):
        mine = jnp.logical_and(target == ex, asker == col)

        @pl.when(jnp.logical_and(wanted, jnp.logical_not(mine)))
        def _():
            query_copy(target).start()

        @pl.when(jnp.logical_and(wanted, mine))
        def _():
            keep_query().start()

    def lower_planes():
        @pl.when(has_lower)
        def _():
            pl.semaphore_wait(ready_sem.at[0], 1)
            pl.when(has_upper)(lambda: signal_plane(ready_sem.at[0], 1))

        for target in range(n_ex):
            send_query(target, target <= ex)

    def upper_planes(here):
        @pl.when(jnp.logical_and(here, has_upper))
        def _():
            pl.semaphore_wait(ready_sem.at[1], 1)
            pl.when(has_lower)(lambda: signal_plane(ready_sem.at[1], -1))

        for target in range(n_ex):
            send_query(target, jnp.logical_and(here, target > ex))

    offsets = [
        (dl, dc) for dl in range(n_lay) for dc in range(0, n_col, 2) if dl or dc
    ]
    offsets.sort(key=lambda at: (at[0] != 0) + (at[1] != 0))

    def piece_copy(number, dl, dc):
        to_lay, to_col = lax.rem(lay + dl, n_lay), lax.rem(col + dc, n_col)
        return pltpu.make_async_remote_copy(
            src_ref=owned_ref.at[to_lay],
            dst_ref=pieces_ref.at[lay, col],
            send_sem=piece_send.at[number],
            recv_sem=piece_recv.at[lay, col],
            device_id={"ex": ex, "col": to_col, "lay": to_lay},
            device_id_type=MESH,
        )

    def relay_copy(number, source, at_lay, at_col):
        return pltpu.make_async_remote_copy(
            src_ref=source,
            dst_ref=pieces_ref.at[at_lay, at_col],
            send_sem=relay_send.at[number],
            recv_sem=piece_recv.at[at_lay, at_col],
            device_id={"ex": ex, "col": sibling, "lay": lay},
            device_id_type=MESH,
        )

    def arrive(at_lay, at_col):
        pltpu.make_async_remote_copy(
            src_ref=owned_ref.at[0],
            dst_ref=pieces_ref.at[at_lay, at_col],
            send_sem=relay_send.at[0],
            recv_sem=piece_recv.at[at_lay, at_col],
            device_id={"ex": ex, "col": sibling, "lay": lay},
            device_id_type=MESH,
        ).wait_recv()

    sends = [piece_copy(n, dl, dc) for n, (dl, dc) in enumerate(offsets)]
    for copy in sends:
        copy.start()
    own_relay = relay_copy(len(offsets), owned_ref.at[lay], lay, col)
    own_relay.start()
    sends.append(own_relay)

    lower_planes()

    tabs_ref[col] = own_tab_ref[...]
    for dc in range(1, n_col):
        source = lax.rem(col + dc, n_col)
        pltpu.make_async_remote_copy(
            src_ref=own_tab_ref,
            dst_ref=tabs_ref.at[source],
            send_sem=tab_send.at[dc],
            recv_sem=tab_recv.at[source],
            device_id={"ex": ex, "col": source, "lay": lay},
            device_id_type=MESH,
        ).wait_recv()

    def table(at_lay, at_col, first, count):
        targets = (first + lax.broadcasted_iota(jnp.int32, (count, LANES), 0)).astype(jnp.float32)
        value = jnp.zeros((count, LANES), jnp.float32)
        for k in range(k_sel):
            index = tabs_ref[at_col, at_lay, k : k + 1, :]
            gain = tabs_ref[at_col, at_lay, k_sel + k : k_sel + k + 1, :]
            value = value + jnp.where(targets == index, gain, 0.0)
        return value

    for at_lay in range(layers):
        for at_col in range(n_col):
            mine = table(at_lay, at_col, col * out_blocks, out_blocks) * scale
            for b in range(in_blocks):
                splat_ref[at_lay, at_col, b] = jnp.broadcast_to(
                    mine[:, b : b + 1], (out_blocks, LANES)
                )

    def rotate(source, at_lay, at_col):
        piece = source[...]
        stacked = jnp.concatenate(
            [piece[:, b * LANES : (b + 1) * LANES] for b in range(in_blocks)], axis=0
        )
        rot_ref[at_lay, at_col] = jnp.dot(
            stacked, had_ref[...], preferred_element_type=jnp.float32
        ).reshape(in_blocks, rows, LANES)

    group = 4

    def combine(at_lay, at_col, first, last):
        for o in range(0, out_blocks, group):
            if first:
                sums = [jnp.zeros((rows, LANES), jnp.float32) for _ in range(group)]
            else:
                sums = [total_ref[o + g] for g in range(group)]
            for b in range(in_blocks):
                turned = rot_ref[at_lay, at_col, b]
                for g in range(group):
                    sums[g] = sums[g] + turned * splat_ref[at_lay, at_col, b, o + g : o + g + 1, :]
            for g in range(group):
                if last:
                    sketch_ref[:, (o + g) * LANES : (o + g + 1) * LANES] = sums[g].astype(
                        jnp.bfloat16
                    )
                else:
                    total_ref[o + g] = sums[g]

    rotate(owned_ref.at[lay], lay, col)
    combine(lay, col, True, False)

    for at_lay in range(layers):
        for at_col in range(n_col):
            whole = table(at_lay, at_col, 0, n_col * out_blocks).T
            turned_tab_ref[at_lay, at_col] = whole[0:padded].astype(jnp.bfloat16)

    arrive(lay, sibling)
    rotate(pieces_ref.at[lay, sibling], lay, sibling)
    combine(lay, sibling, False, False)
    upper_planes(has_lower)
    relays = []
    for number, (dl, dc) in enumerate(offsets):
        if number == len(offsets) - 1:
            upper_planes(jnp.logical_not(has_lower))
        at_lay, at_col = lax.rem(lay + dl, n_lay), lax.rem(col + dc, n_col)
        arrive(at_lay, at_col)
        relay = relay_copy(number, pieces_ref.at[at_lay, at_col], at_lay, at_col)
        relay.start()
        relays.append(relay)
        rotate(pieces_ref.at[at_lay, at_col], at_lay, at_col)
        combine(at_lay, at_col, False, False)
    for number, (dl, dc) in enumerate(offsets):
        at_lay, at_col = lax.rem(lay + dl, n_lay), lax.rem(sibling + dc, n_col)
        last = number == len(offsets) - 1
        arrive(at_lay, at_col)
        rotate(pieces_ref.at[at_lay, at_col], at_lay, at_col)
        combine(at_lay, at_col, False, last)

    for j in range(per_col):
        holder = col * per_col + j
        for other in range(n_col):
            here = jnp.logical_and(holder == ex, other == col)

            @pl.when(jnp.logical_not(here))
            def _():
                pltpu.make_async_remote_copy(
                    src_ref=own_query_ref,
                    dst_ref=queries_ref.at[j, other],
                    send_sem=query_send.at[0],
                    recv_sem=query_recv.at[j, other],
                    device_id={"ex": holder, "col": other, "lay": lay},
                    device_id_type=MESH,
                ).wait_recv()

            @pl.when(here)
            def _():
                keep_query().wait()

    asked = jnp.concatenate(
        [
            queries_ref[j].astype(jnp.float32).reshape(n_col * out_blocks, LANES)
            for j in range(per_col)
        ],
        axis=1,
    ).astype(jnp.bfloat16)
    weights_ref[...] = jnp.dot(
        turned_tab_ref[...].reshape(layers * n_col * padded, n_col * out_blocks),
        asked,
        preferred_element_type=jnp.float32,
    ).reshape(weights_ref.shape)
    for q in range(per_col):
        sums = jnp.zeros((rows, LANES), jnp.float32)
        for at_lay in range(layers):
            for at_col in range(n_col):
                for b in range(in_blocks):
                    sums = sums + rot_ref[at_lay, at_col, b] * weights_ref[
                        at_lay, at_col, b : b + 1, q * LANES : (q + 1) * LANES
                    ]
        scores_ref[q : q + 1, :] = jnp.sum(sums.T, axis=0, keepdims=True) * scale

    for copy in sends + relays + tab_copies:
        copy.wait_send()
    for target in range(n_ex):
        mine = jnp.logical_and(target == ex, asker == col)

        @pl.when(jnp.logical_not(mine))
        def _():
            query_copy(target).wait_send()


def solution(mesh):
    n_ex, n_col, n_lay = (mesh.shape[name] for name in ("ex", "col", "lay"))

    def local(normalized, upstream, owner_order, sketch_index, sketch_scale, query_sketch):
        examples, own_layers, tokens, features = normalized.shape
        assert own_layers == 1
        layers, in_blocks, k_sel = sketch_index.shape
        width = query_sketch.shape[1]
        out_blocks = width // LANES
        per_col = n_ex * query_sketch.shape[0] // n_col
        rows = examples // n_lay
        padded = -(-in_blocks // 16) * 16
        vmem = pl.BlockSpec(memory_space=pltpu.VMEM)
        dma = pltpu.SemaphoreType.DMA
        sketch, scores = pl.pallas_call(
            functools.partial(kernel, (n_ex, n_col, n_lay, per_col, k_sel)),
            out_shape=(
                pltpu.VMEM((rows, width), jnp.bfloat16),
                pltpu.VMEM((per_col, rows), jnp.float32),
            ),
            in_specs=[pl.BlockSpec(memory_space=pl.ANY)] * 6,
            out_specs=(vmem, vmem),
            scratch_shapes=[
                pltpu.VMEM(owner_order.shape, jnp.int32),
                pltpu.VMEM((layers, k_sel, in_blocks), jnp.int32),
                pltpu.VMEM((layers, k_sel, in_blocks), jnp.bfloat16),
                pltpu.VMEM(query_sketch.shape, jnp.bfloat16),
                pltpu.VMEM((examples, tokens, features), jnp.bfloat16),
                pltpu.VMEM((examples, tokens, features), jnp.bfloat16),
                pltpu.VMEM((examples, features), jnp.bfloat16),
                pltpu.VMEM((n_lay, rows, features), jnp.bfloat16),
                pltpu.VMEM((n_lay, n_col, rows, features), jnp.bfloat16),
                pltpu.VMEM((layers, 2 * k_sel, LANES), jnp.float32),
                pltpu.VMEM((n_col, layers, 2 * k_sel, LANES), jnp.float32),
                pltpu.VMEM((out_blocks, LANES), jnp.float32),
                pltpu.VMEM((out_blocks, LANES), jnp.bfloat16),
                pltpu.VMEM((per_col, n_col, out_blocks, LANES), jnp.bfloat16),
                pltpu.VMEM((LANES, LANES), jnp.bfloat16),
                pltpu.VMEM((layers, n_col, in_blocks, out_blocks, LANES), jnp.float32),
                pltpu.VMEM((layers, n_col, padded, n_col * out_blocks), jnp.bfloat16),
                pltpu.VMEM((layers, n_col, padded, per_col * LANES), jnp.float32),
                pltpu.VMEM((n_lay, n_col, in_blocks, rows, LANES), jnp.float32),
                pltpu.VMEM((out_blocks, rows, LANES), jnp.float32),
                dma((2 * CHUNKS,)),
                dma((4,)),
                dma((n_lay * n_col,)),
                dma((n_lay, n_col)),
                dma((n_lay * n_col,)),
                dma((n_col,)),
                dma((n_col,)),
                dma((n_ex,)),
                dma((per_col, n_col)),
                pltpu.SemaphoreType.REGULAR((2,)),
            ],
            compiler_params=pltpu.CompilerParams(collective_id=0, has_side_effects=True),
        )(
            normalized.reshape(examples, tokens, features),
            upstream.reshape(examples, tokens, features),
            owner_order,
            jnp.swapaxes(sketch_index, 1, 2),
            jnp.swapaxes(sketch_scale, 1, 2),
            query_sketch,
        )
        return sketch, scores.T

    placed = (
        P("ex", "lay", None, "col"),
        P("ex", "lay", None, "col"),
        P("ex", None),
        P(None, "col", None),
        P(None, "col", None),
        P("ex", "col"),
    )
    return jax.shard_map(
        local,
        mesh=mesh,
        in_specs=placed,
        out_specs=(P(("ex", "lay"), "col"), P(("ex", "lay"), "col")),
        check_vma=False,
    )
```

```python
import functools
import math

import jax
import jax.numpy as jnp
from jax import lax
from jax.experimental import pallas as pl
from jax.experimental.pallas import tpu as pltpu
from jax.sharding import PartitionSpec as P

MESH = pl.DeviceIdType.MESH
LANES = 128
CHUNKS = 4


def signs():
    bits = lax.broadcasted_iota(jnp.int32, (LANES, LANES), 0) & lax.broadcasted_iota(
        jnp.int32, (LANES, LANES), 1
    )
    bits = bits ^ (bits >> 4)
    bits = bits ^ (bits >> 2)
    bits = bits ^ (bits >> 1)
    return (1 - 2 * (bits & 1)).astype(jnp.float32).astype(jnp.bfloat16)


def kernel(
    sizes,
    x_hbm,
    u_hbm,
    order_hbm,
    index_hbm,
    scale_hbm,
    query_hbm,
    sketch_ref,
    scores_ref,
    order_ref,
    index_ref,
    scale_ref,
    query_ref,
    x_ref,
    u_ref,
    grads_ref,
    owned_ref,
    pieces_ref,
    own_tab_ref,
    tabs_ref,
    own_query_f32_ref,
    own_query_ref,
    queries_ref,
    had_ref,
    splat_ref,
    turned_tab_ref,
    weights_ref,
    rot_ref,
    total_ref,
    in_sem,
    small_sem,
    piece_send,
    piece_recv,
    relay_send,
    tab_send,
    tab_recv,
    query_send,
    query_recv,
    ready_sem,
):
    n_ex, n_col, n_lay, per_col, k_sel = sizes
    ex, col, lay = lax.axis_index("ex"), lax.axis_index("col"), lax.axis_index("lay")
    examples, tokens, features = x_ref.shape
    rows = examples // n_lay
    in_blocks = features // LANES
    layers = index_ref.shape[0]
    out_blocks = query_ref.shape[1] // LANES
    padded = weights_ref.shape[2]
    chunk = examples // CHUNKS
    sibling = col + 1 - 2 * lax.rem(col, 2)
    scale = 1.0 / math.sqrt(float(LANES))

    loads = []
    for i in range(CHUNKS):
        part = pl.ds(i * chunk, chunk)
        pair = [
            pltpu.make_async_copy(x_hbm.at[part], x_ref.at[part], in_sem.at[2 * i]),
            pltpu.make_async_copy(u_hbm.at[part], u_ref.at[part], in_sem.at[2 * i + 1]),
        ]
        for copy in pair:
            copy.start()
        loads.append(pair)

    smalls = [
        pltpu.make_async_copy(source, held, small_sem.at[i])
        for i, (source, held) in enumerate(
            [
                (query_hbm, query_ref),
                (index_hbm, index_ref),
                (scale_hbm, scale_ref),
                (order_hbm, order_ref),
            ]
        )
    ]
    for copy in smalls:
        copy.start()

    barrier = pltpu.get_barrier_semaphore()
    for dl in range(n_lay):
        for dc in range(n_col):
            if dl or dc:
                pl.semaphore_signal(
                    barrier,
                    inc=1,
                    device_id={
                        "ex": ex,
                        "col": lax.rem(col + dc, n_col),
                        "lay": lax.rem(lay + dl, n_lay),
                    },
                    device_id_type=MESH,
                )
    has_lower, has_upper = ex > 0, ex < n_ex - 1

    def signal_plane(sem, step):
        pl.semaphore_signal(
            sem,
            inc=1,
            device_id={"ex": ex + step, "col": col, "lay": lay},
            device_id_type=MESH,
        )

    pl.when(has_lower)(lambda: signal_plane(barrier, -1))
    pl.when(has_upper)(lambda: signal_plane(barrier, 1))

    had_ref[...] = signs()
    for copy in smalls:
        copy.wait()
    own_tab_ref[...] = jnp.full(own_tab_ref.shape, -1.0, jnp.float32)
    for layer in range(layers):
        own_tab_ref[layer, 0:k_sel, 0:in_blocks] = index_ref[layer].astype(jnp.float32)
        own_tab_ref[layer, k_sel : 2 * k_sel, 0:in_blocks] = scale_ref[layer].astype(jnp.float32)
    for o in range(out_blocks):
        own_query_f32_ref[o : o + 1, :] = query_ref[:, o * LANES : (o + 1) * LANES].astype(
            jnp.float32
        )
    own_query_ref[...] = own_query_f32_ref[...].astype(jnp.bfloat16)

    def tab_copy(dc):
        return pltpu.make_async_remote_copy(
            src_ref=own_tab_ref,
            dst_ref=tabs_ref.at[col],
            send_sem=tab_send.at[dc],
            recv_sem=tab_recv.at[col],
            device_id={"ex": ex, "col": lax.rem(col + dc, n_col), "lay": lay},
            device_id_type=MESH,
        )

    for i in range(CHUNKS):
        if i == CHUNKS // 2:
            planes = has_lower.astype(jnp.int32) + has_upper.astype(jnp.int32)
            pl.semaphore_wait(barrier, n_lay * n_col - 1 + planes)
            pl.when(jnp.logical_not(has_lower))(lambda: signal_plane(ready_sem.at[0], 1))
            pl.when(jnp.logical_not(has_upper))(lambda: signal_plane(ready_sem.at[1], -1))
            tab_copies = [tab_copy(dc) for dc in range(1, n_col)]
            for copy in tab_copies:
                copy.start()

        for copy in loads[i]:
            copy.wait()
        part = slice(i * chunk, (i + 1) * chunk)
        grads_ref[part, :] = jnp.sum(
            x_ref[part].astype(jnp.float32) * u_ref[part].astype(jnp.float32), axis=1
        ).astype(jnp.bfloat16)
    chosen = (
        lax.broadcasted_iota(jnp.int32, (examples, examples), 0) == order_ref[...]
    ).astype(jnp.float32)
    chosen = chosen.T.astype(jnp.bfloat16)
    ordered = jnp.dot(chosen, grads_ref[...], preferred_element_type=jnp.float32)
    for owner in range(n_lay):
        owned_ref[owner] = ordered[owner * rows : (owner + 1) * rows].astype(jnp.bfloat16)

    asker = ex // per_col
    slot = lax.rem(ex, per_col)

    def query_copy(target):
        return pltpu.make_async_remote_copy(
            src_ref=own_query_ref,
            dst_ref=queries_ref.at[slot, col],
            send_sem=query_send.at[target],
            recv_sem=query_recv.at[slot, col],
            device_id={"ex": target, "col": asker, "lay": lay},
            device_id_type=MESH,
        )

    def keep_query():
        return pltpu.make_async_copy(
            own_query_ref, queries_ref.at[slot, col], query_recv.at[slot, col]
        )

    def send_query(target, wanted):
        mine = jnp.logical_and(target == ex, asker == col)

        @pl.when(jnp.logical_and(wanted, jnp.logical_not(mine)))
        def _():
            query_copy(target).start()

        @pl.when(jnp.logical_and(wanted, mine))
        def _():
            keep_query().start()

    def lower_planes():
        @pl.when(has_lower)
        def _():
            pl.semaphore_wait(ready_sem.at[0], 1)
            pl.when(has_upper)(lambda: signal_plane(ready_sem.at[0], 1))

        for target in range(n_ex):
            send_query(target, target <= ex)

    def upper_planes(here):
        @pl.when(jnp.logical_and(here, has_upper))
        def _():
            pl.semaphore_wait(ready_sem.at[1], 1)
            pl.when(has_lower)(lambda: signal_plane(ready_sem.at[1], -1))

        for target in range(n_ex):
            send_query(target, jnp.logical_and(here, target > ex))

    offsets = [
        (dl, dc) for dl in range(n_lay) for dc in range(0, n_col, 2) if dl or dc
    ]
    offsets.sort(key=lambda at: (at[0] != 0) + (at[1] != 0))

    def piece_copy(number, dl, dc):
        to_lay, to_col = lax.rem(lay + dl, n_lay), lax.rem(col + dc, n_col)
        return pltpu.make_async_remote_copy(
            src_ref=owned_ref.at[to_lay],
            dst_ref=pieces_ref.at[lay, col],
            send_sem=piece_send.at[number],
            recv_sem=piece_recv.at[lay, col],
            device_id={"ex": ex, "col": to_col, "lay": to_lay},
            device_id_type=MESH,
        )

    def relay_copy(number, source, at_lay, at_col):
        return pltpu.make_async_remote_copy(
            src_ref=source,
            dst_ref=pieces_ref.at[at_lay, at_col],
            send_sem=relay_send.at[number],
            recv_sem=piece_recv.at[at_lay, at_col],
            device_id={"ex": ex, "col": sibling, "lay": lay},
            device_id_type=MESH,
        )

    def arrive(at_lay, at_col):
        pltpu.make_async_remote_copy(
            src_ref=owned_ref.at[0],
            dst_ref=pieces_ref.at[at_lay, at_col],
            send_sem=relay_send.at[0],
            recv_sem=piece_recv.at[at_lay, at_col],
            device_id={"ex": ex, "col": sibling, "lay": lay},
            device_id_type=MESH,
        ).wait_recv()

    sends = [piece_copy(n, dl, dc) for n, (dl, dc) in enumerate(offsets)]
    for copy in reversed(sends):
        copy.start()
    own_relay = relay_copy(len(offsets), owned_ref.at[lay], lay, col)
    own_relay.start()
    sends.append(own_relay)

    lower_planes()
    upper_planes(has_lower)

    tabs_ref[col] = own_tab_ref[...]
    for dc in range(1, n_col):
        source = lax.rem(col + dc, n_col)
        pltpu.make_async_remote_copy(
            src_ref=own_tab_ref,
            dst_ref=tabs_ref.at[source],
            send_sem=tab_send.at[dc],
            recv_sem=tab_recv.at[source],
            device_id={"ex": ex, "col": source, "lay": lay},
            device_id_type=MESH,
        ).wait_recv()

    def table(at_lay, at_col, first, count):
        targets = (first + lax.broadcasted_iota(jnp.int32, (count, LANES), 0)).astype(jnp.float32)
        value = jnp.zeros((count, LANES), jnp.float32)
        for k in range(k_sel):
            index = tabs_ref[at_col, at_lay, k : k + 1, :]
            gain = tabs_ref[at_col, at_lay, k_sel + k : k_sel + k + 1, :]
            value = value + jnp.where(targets == index, gain, 0.0)
        return value

    for at_lay in range(layers):
        for at_col in range(n_col):
            mine = table(at_lay, at_col, col * out_blocks, out_blocks) * scale
            for b in range(in_blocks):
                splat_ref[at_lay, at_col, b] = jnp.broadcast_to(
                    mine[:, b : b + 1], (out_blocks, LANES)
                )

    def rotate(source, at_lay, at_col):
        piece = source[...]
        stacked = jnp.concatenate(
            [piece[:, b * LANES : (b + 1) * LANES] for b in range(in_blocks)], axis=0
        )
        rot_ref[at_lay, at_col] = jnp.dot(
            stacked, had_ref[...], preferred_element_type=jnp.float32
        ).reshape(in_blocks, rows, LANES)

    group = 4

    def combine(at_lay, at_col, first, last):
        for o in range(0, out_blocks, group):
            if first:
                sums = [jnp.zeros((rows, LANES), jnp.float32) for _ in range(group)]
            else:
                sums = [total_ref[o + g] for g in range(group)]
            for b in range(in_blocks):
                turned = rot_ref[at_lay, at_col, b]
                for g in range(group):
                    sums[g] = sums[g] + turned * splat_ref[at_lay, at_col, b, o + g : o + g + 1, :]
            for g in range(group):
                if last:
                    sketch_ref[:, (o + g) * LANES : (o + g + 1) * LANES] = sums[g].astype(
                        jnp.bfloat16
                    )
                else:
                    total_ref[o + g] = sums[g]

    rotate(owned_ref.at[lay], lay, col)
    combine(lay, col, True, False)

    for at_lay in range(layers):
        for at_col in range(n_col):
            whole = table(at_lay, at_col, 0, n_col * out_blocks).T
            turned_tab_ref[at_lay, at_col] = whole[0:padded].astype(jnp.bfloat16)

    arrive(lay, sibling)
    rotate(pieces_ref.at[lay, sibling], lay, sibling)
    combine(lay, sibling, False, False)
    upper_planes(jnp.logical_not(has_lower))
    relays = []
    for number, (dl, dc) in enumerate(offsets):
        at_lay, at_col = lax.rem(lay + dl, n_lay), lax.rem(col + dc, n_col)
        arrive(at_lay, at_col)
        relay = relay_copy(number, pieces_ref.at[at_lay, at_col], at_lay, at_col)
        relay.start()
        relays.append(relay)
        rotate(pieces_ref.at[at_lay, at_col], at_lay, at_col)
        combine(at_lay, at_col, False, False)
    for number, (dl, dc) in enumerate(offsets):
        at_lay, at_col = lax.rem(lay + dl, n_lay), lax.rem(sibling + dc, n_col)
        last = number == len(offsets) - 1
        arrive(at_lay, at_col)
        rotate(pieces_ref.at[at_lay, at_col], at_lay, at_col)
        combine(at_lay, at_col, False, last)

    for j in range(per_col):
        holder = col * per_col + j
        for other in range(n_col):
            here = jnp.logical_and(holder == ex, other == col)

            @pl.when(jnp.logical_not(here))
            def _():
                pltpu.make_async_remote_copy(
                    src_ref=own_query_ref,
                    dst_ref=queries_ref.at[j, other],
                    send_sem=query_send.at[0],
                    recv_sem=query_recv.at[j, other],
                    device_id={"ex": holder, "col": other, "lay": lay},
                    device_id_type=MESH,
                ).wait_recv()

            @pl.when(here)
            def _():
                keep_query().wait()

    asked = jnp.concatenate(
        [
            queries_ref[j].astype(jnp.float32).reshape(n_col * out_blocks, LANES)
            for j in range(per_col)
        ],
        axis=1,
    ).astype(jnp.bfloat16)
    weights_ref[...] = jnp.dot(
        turned_tab_ref[...].reshape(layers * n_col * padded, n_col * out_blocks),
        asked,
        preferred_element_type=jnp.float32,
    ).reshape(weights_ref.shape)
    for q in range(per_col):
        sums = jnp.zeros((rows, LANES), jnp.float32)
        for at_lay in range(layers):
            for at_col in range(n_col):
                for b in range(in_blocks):
                    sums = sums + rot_ref[at_lay, at_col, b] * weights_ref[
                        at_lay, at_col, b : b + 1, q * LANES : (q + 1) * LANES
                    ]
        scores_ref[q : q + 1, :] = jnp.sum(sums.T, axis=0, keepdims=True) * scale

    for copy in sends + relays + tab_copies:
        copy.wait_send()
    for target in range(n_ex):
        mine = jnp.logical_and(target == ex, asker == col)

        @pl.when(jnp.logical_not(mine))
        def _():
            query_copy(target).wait_send()


def solution(mesh):
    n_ex, n_col, n_lay = (mesh.shape[name] for name in ("ex", "col", "lay"))

    def local(normalized, upstream, owner_order, sketch_index, sketch_scale, query_sketch):
        examples, own_layers, tokens, features = normalized.shape
        assert own_layers == 1
        layers, in_blocks, k_sel = sketch_index.shape
        width = query_sketch.shape[1]
        out_blocks = width // LANES
        per_col = n_ex * query_sketch.shape[0] // n_col
        rows = examples // n_lay
        padded = -(-in_blocks // 16) * 16
        vmem = pl.BlockSpec(memory_space=pltpu.VMEM)
        dma = pltpu.SemaphoreType.DMA
        sketch, scores = pl.pallas_call(
            functools.partial(kernel, (n_ex, n_col, n_lay, per_col, k_sel)),
            out_shape=(
                pltpu.VMEM((rows, width), jnp.bfloat16),
                pltpu.VMEM((per_col, rows), jnp.float32),
            ),
            in_specs=[pl.BlockSpec(memory_space=pl.ANY)] * 6,
            out_specs=(vmem, vmem),
            scratch_shapes=[
                pltpu.VMEM(owner_order.shape, jnp.int32),
                pltpu.VMEM((layers, k_sel, in_blocks), jnp.int32),
                pltpu.VMEM((layers, k_sel, in_blocks), jnp.bfloat16),
                pltpu.VMEM(query_sketch.shape, jnp.bfloat16),
                pltpu.VMEM((examples, tokens, features), jnp.bfloat16),
                pltpu.VMEM((examples, tokens, features), jnp.bfloat16),
                pltpu.VMEM((examples, features), jnp.bfloat16),
                pltpu.VMEM((n_lay, rows, features), jnp.bfloat16),
                pltpu.VMEM((n_lay, n_col, rows, features), jnp.bfloat16),
                pltpu.VMEM((layers, 2 * k_sel, LANES), jnp.float32),
                pltpu.VMEM((n_col, layers, 2 * k_sel, LANES), jnp.float32),
                pltpu.VMEM((out_blocks, LANES), jnp.float32),
                pltpu.VMEM((out_blocks, LANES), jnp.bfloat16),
                pltpu.VMEM((per_col, n_col, out_blocks, LANES), jnp.bfloat16),
                pltpu.VMEM((LANES, LANES), jnp.bfloat16),
                pltpu.VMEM((layers, n_col, in_blocks, out_blocks, LANES), jnp.float32),
                pltpu.VMEM((layers, n_col, padded, n_col * out_blocks), jnp.bfloat16),
                pltpu.VMEM((layers, n_col, padded, per_col * LANES), jnp.float32),
                pltpu.VMEM((n_lay, n_col, in_blocks, rows, LANES), jnp.float32),
                pltpu.VMEM((out_blocks, rows, LANES), jnp.float32),
                dma((2 * CHUNKS,)),
                dma((4,)),
                dma((n_lay * n_col,)),
                dma((n_lay, n_col)),
                dma((n_lay * n_col,)),
                dma((n_col,)),
                dma((n_col,)),
                dma((n_ex,)),
                dma((per_col, n_col)),
                pltpu.SemaphoreType.REGULAR((2,)),
            ],
            compiler_params=pltpu.CompilerParams(collective_id=0, has_side_effects=True),
        )(
            normalized.reshape(examples, tokens, features),
            upstream.reshape(examples, tokens, features),
            owner_order,
            jnp.swapaxes(sketch_index, 1, 2),
            jnp.swapaxes(sketch_scale, 1, 2),
            query_sketch,
        )
        return sketch, scores.T

    placed = (
        P("ex", "lay", None, "col"),
        P("ex", "lay", None, "col"),
        P("ex", None),
        P(None, "col", None),
        P(None, "col", None),
        P("ex", "col"),
    )
    return jax.shard_map(
        local,
        mesh=mesh,
        in_specs=placed,
        out_specs=(P(("ex", "lay"), "col"), P(("ex", "lay"), "col")),
        check_vma=False,
    )
```
